32 devices in a mesh: row: 4 (over z), col: 8 (over y, x, core).
Axes of the slice: x: 2, y: 2, z: 4, core: 2. Of those that a mesh axis runs over, the one named last changes fastest.
Arguments:
- factor_panel: bfloat16 [1024, 8192], P('row', 'col'), may hold values from -0.1875 to 0.1875
- ancestor_inv: float32 [1024, 1024], P('row', 'col'), may hold values from -6 to 6
- diag_inverse: float32 [4096, 8192], P('row', 'col'), may hold values from -6 to 6
- structure: int32 [2, 4], replicated, may hold values 0 or 1
Outputs:
- inverse_panel: float32 [1024, 8192], P('row', 'col')
- diag_sigma: float32 [4096, 8192], P('row', 'col')
The draws below stay inside these ranges and needn't reach their ends.
All inputs are finite; a program needn't handle non-finite values.
Results may differ from the reference program's by a relative error of at most 0.0003.
Values may be sent and summed in bfloat16 or wider, within the bound.
A program may use at most 128 MiB of HBM per device.

```python
import jax
import jax.numpy as jnp
from jax import lax

B = 256
W = 4096
NS = 2
NA = 1024
NT = 4
N_COL = 8


def with_ends(values, stream_key, smallest, high):
    longest = values.shape.index(max(values.shape))
    spots = []
    for shift in (0, 1):
        where = [jax.random.randint(jax.random.fold_in(stream_key, axis), (), 0, length) for axis, length in enumerate(values.shape)]
        where[longest] = (where[longest] + shift) % values.shape[longest]
        spots.append(tuple(where))
    return values.at[spots[0]].set(smallest).at[spots[1]].set(high)


def shard_levels(key, dims, split, low, largest):
    factor_of, own = 1.0, jax.random.fold_in(key, 6)
    for dim, blocks in split:
        steps = jnp.exp(jax.random.uniform(jax.random.fold_in(own, dim), (blocks,), jnp.float32, low / len(split), largest / len(split)))
        factor_of = factor_of * jnp.repeat(steps, dims[dim] // blocks).reshape([-1 if axis == dim else 1 for axis in range(len(dims))])
    return factor_of


def normal_values(own_key, shape, spread, reach, cuts=(), kind=jnp.bfloat16):
    array = spread * jax.random.normal(own_key, shape, jnp.float32)
    if cuts:
        array = array * shard_levels(own_key, shape, cuts, -0.22, 0.18)
    return jnp.clip(array, -reach, reach).astype(kind)


def setup_inputs(seed: int = 0) -> dict:
    seeds = jax.random.split(jax.random.key(seed), 5)
    factor_panel = normal_values(seeds[0], (NA, NS * W), NA ** -0.5, 0.1875, ((0, 4), (1, 8)))
    ancestor_inv = normal_values(seeds[1], (NA, NA), 1.0, 6.0, ((0, 4), (1, 8)), jnp.float32)
    diag_inverse = normal_values(seeds[2], (W, NS * W), 1.0, 6.0, ((0, 4), (1, 8)), jnp.float32)
    structure = with_ends((jax.random.randint(seeds[3], (NS, NT), 0, 4) < 3).astype(jnp.int32), jax.random.fold_in(seeds[3], 1), 0, 1)
    return {"factor_panel": factor_panel, "ancestor_inv": ancestor_inv, "diag_inverse": diag_inverse, "structure": structure}


def reference(factor_panel, ancestor_inv, diag_inverse, structure):
    per_block = W // N_COL
    panel_cube = factor_panel.reshape(NA, N_COL, NS, per_block)
    diag_cube = diag_inverse.reshape(W, N_COL, NS, per_block)
    panels = []
    blocks = []
    for member in range(NS):
        keep = jnp.repeat(structure[member], B) == 1
        window = panel_cube[:, :, member, :].reshape(NA, W)
        lhat = jnp.where(keep[:, None], window, jnp.zeros_like(window))
        lhat_wide = lhat.astype(jnp.float32)
        product = jnp.dot(ancestor_inv, lhat_wide, precision=lax.Precision.HIGHEST)
        inverse_part = jnp.where(keep[:, None], -product, jnp.zeros_like(product))
        update = jnp.dot(lhat_wide.T, inverse_part, precision=lax.Precision.HIGHEST)
        panels.append(inverse_part.reshape(NA, N_COL, per_block))
        blocks.append((diag_cube[:, :, member, :].reshape(W, W) - update).reshape(W, N_COL, per_block))
    inverse_panel = jnp.stack(panels, axis=2).reshape(NA, NS * W)
    diag_sigma = jnp.stack(blocks, axis=2).reshape(W, NS * W)
    return inverse_panel, diag_sigma
```

```python
import functools

import jax
import jax.numpy as jnp
from jax import lax
from jax.experimental import pallas as pl
from jax.experimental.pallas import tpu as pltpu
from jax.sharding import PartitionSpec as P

B = 256
NS = 2
NR = 4
NC = 8
MESH = pl.DeviceIdType.MESH


def local(factor_panel, ancestor_inv, diag_inverse, structure):
    rows_dev, width_dev = factor_panel.shape
    per_block = width_dev // NS
    row_index = lax.axis_index("row")
    keep_tiles = jnp.repeat(structure, B, axis=1)
    keep_own = lax.dynamic_slice_in_dim(keep_tiles, row_index * rows_dev, rows_dev, 1)
    keep_cols = jnp.repeat(keep_own.T, per_block, axis=1)
    lhat_local = jnp.where(keep_cols == 1, factor_panel, jnp.zeros_like(factor_panel))
    column = lax.all_gather(lhat_local, "row", axis=0, tiled=True)
    sigma_rows = lax.all_gather(ancestor_inv, "col", axis=1, tiled=True)
    column_wide = column.astype(jnp.float32)
    running = jnp.dot(sigma_rows, column_wide, precision=lax.Precision.HIGHEST)
    inverse_panel = jnp.where(keep_cols == 1, -running, jnp.zeros_like(running))
    rows_all = lax.all_gather(lhat_local, "col", axis=1, tiled=True)
    block_count = rows_all.shape[1] // width_dev
    rows_cube = rows_all.reshape(rows_dev, block_count, NS, per_block)
    lhat_members = [
        rows_cube[:, :, member, :].reshape(rows_dev, block_count * per_block).astype(jnp.float32)
        for member in range(NS)
    ]
    pieces = []
    for member in range(NS):
        window = lhat_members[member]
        target = inverse_panel[:, member * per_block : (member + 1) * per_block]
        pieces.append(
            lax.dot_general(
                window,
                target,
                (((0,), (0,)), ((), ())),
                precision=lax.Precision.HIGHEST,
                preferred_element_type=jnp.float32,
            )
        )
    update = lax.psum_scatter(
        jnp.concatenate(pieces, axis=1), "row", scatter_dimension=0, tiled=True
    )
    diag_sigma = diag_inverse - update
    return (inverse_panel, diag_sigma)


def kernel(structure, factor, anc, diag_in, panel_out, diag_out,
           lt, pr, asl, a_hi, a_lo, q_hi, q_lo, diag_v,
           zl_send, zl_recv, za_send, za_recv, ra_send, ra_recv, sa_send, sa_recv,
           pc_send, pc_recv, ps_send, ps_recv, lc_sem, di_sem, do_sem):
    r = lax.axis_index("row")
    c = lax.axis_index("col")
    wide = factor.shape[1] // NS
    rows = factor.shape[0]
    acols = anc.shape[1]
    core = lax.rem(c, 2)
    pos = c // 2
    step = 1 - 2 * core

    def ring_of(p):
        y = p // 2
        return 2 * y + lax.rem(lax.rem(p, 2) + y, 2)

    def pos_of(q):
        y = q // 2
        return 2 * y + lax.rem(lax.rem(q, 2) + y, 2)

    q_me = ring_of(pos)
    q_src = ring_of(r)
    hop = lax.rem((q_me - q_src) * step + 8, 4)

    def ring_col(k):
        return pos_of(lax.rem(q_me + k * step + 8, 4)) * 2 + core

    nxt, prv = ring_col(1), ring_col(-1)
    sib = pos * 2 + 1 - core
    peers = [(lax.rem(r + d, NR), c) for d in range(1, NR)]

    barrier = pltpu.get_barrier_semaphore()
    for dev in peers + [(r, nxt), (r, prv), (r, sib)]:
        pl.semaphore_signal(barrier, inc=1, device_id=dev, device_id_type=MESH)

    diag_load = pltpu.make_async_copy(diag_in, diag_v, di_sem)
    diag_load.start()
    asl[c, r] = anc[...]
    for s in range(NS):
        part = factor[:, s * wide:(s + 1) * wide]
        kept = jnp.where(structure[s, r] == 1, part.astype(jnp.float32), 0.0)
        lt[r, s] = kept.T.astype(jnp.bfloat16)
    pl.semaphore_wait(barrier, 6)

    def remote(src, dst, send, recv, dev):
        return pltpu.make_async_remote_copy(
            src_ref=src, dst_ref=dst, send_sem=send, recv_sem=recv,
            device_id=dev, device_id_type=MESH)

    sends = []

    def go(*args):
        copy = remote(*args)
        copy.start()
        sends.append(copy)

    for d in range(NR - 1):
        go(asl.at[c, r], asl.at[c, r], za_send.at[d], za_recv.at[r], peers[d])
    for s in range(NS):
        for d in range(NR - 1):
            go(lt.at[r, s], lt.at[r, s], zl_send.at[d, s], zl_recv.at[r, s], peers[d])

    turn = 1 - 2 * (r // 2)

    def chain_copy(z, t, s):
        return remote(pr.at[core, z, s], pr.at[core, z, s], pc_send.at[t, s], pc_recv.at[t, s], (r, nxt))

    def sib_copy(z, t, s):
        return remote(pr.at[core, z, s], pr.at[core, z, s], ps_send.at[t, s], ps_recv.at[t, s], (r, sib))

    def wait_lt(t, s):
        z = lax.rem(r + t * turn + 8, NR)
        remote(lt.at[z, s], lt.at[z, s], zl_send.at[0, s], zl_recv.at[z, s], peers[0]).wait_recv()

    def chain(t):
        z = lax.rem(r + t * turn + 8, NR)
        for s in range(NS):
            if t > 0:
                wait_lt(t, s)

            @pl.when(hop == 0)
            def _():
                copy = pltpu.make_async_copy(lt.at[z, s], pr.at[core, z, s], lc_sem.at[t, s])
                copy.start()
                copy.wait()

            @pl.when(hop > 0)
            def _():
                chain_copy(z, t, s).wait_recv()

            @pl.when(hop < 3)
            def _():
                chain_copy(z, t, s).start()

            sib_copy(z, t, s).start()

    def slab(k):
        return ring_col(-k)

    def ring(k):
        col = slab(k)
        if k == 0:
            for d in range(1, NR):
                z = lax.rem(r + d, NR)
                remote(asl.at[c, z], asl.at[c, z], za_send.at[0], za_recv.at[z], peers[0]).wait_recv()
        else:
            remote(asl.at[col], asl.at[col], ra_send.at[k - 1], ra_recv.at[k - 1], (r, nxt)).wait_recv()
        if k < 3:
            go(asl.at[col], asl.at[col], ra_send.at[k], ra_recv.at[k], (r, nxt))
        go(asl.at[col], asl.at[col], sa_send.at[k], sa_recv.at[k], (r, sib))

    def split(col):
        for z in range(NR):
            a = asl[col, z]
            hi = a.astype(jnp.bfloat16)
            a_hi[col, z] = hi
            a_lo[col, z] = (a - hi.astype(jnp.float32)).astype(jnp.bfloat16)

    chain(0)
    ring(0)
    chain(1)
    ring(1)
    ring(2)
    chain(2)
    ring(3)
    for k in range(4):
        other = pos_of(lax.rem(q_me + k * step + 8, 4)) * 2 + 1 - core
        remote(asl.at[other], asl.at[other], sa_send.at[k], sa_recv.at[k], (r, sib)).wait_recv()

    @pl.loop(0, NC)
    def _(col):
        split(col)

    chain(3)

    def dot(a, b, dims):
        return lax.dot_general(a, b, (dims, ((), ())), preferred_element_type=jnp.float32)

    @pl.loop(0, NS * NR)
    def _(it):
        s = it // NR
        z = lax.rem(it, NR)
        rhs = jnp.concatenate([lt[b, s] for b in range(NR)], axis=1)
        hi = jnp.concatenate([a_hi[col, z] for col in range(NC)], axis=1)
        lo = jnp.concatenate([a_lo[col, z] for col in range(NC)], axis=1)
        total = dot(hi, rhs, ((1,), (1,))) + dot(lo, rhs, ((1,), (1,)))
        total = jnp.where(structure[s, z] == 1, -total, 0.0)
        top = total.astype(jnp.bfloat16)
        q_hi[s, z] = top
        q_lo[s, z] = (total - top.astype(jnp.float32)).astype(jnp.bfloat16)
        for m in range(NS):
            @pl.when((z == r) & (s == m))
            def _():
                panel_out[:, m * wide:(m + 1) * wide] = total

    for t in range(NR):
        z = lax.rem(r + t * turn + 8, NR)
        for s in range(NS):
            remote(pr.at[1 - core, z, s], pr.at[1 - core, z, s], ps_send.at[t, s], ps_recv.at[t, s],
                   (r, sib)).wait_recv()
    diag_load.wait()

    half = wide // 2

    for k in range(2):
        @pl.loop(0, 2)
        def _(h):
            for s in range(NS):
                off = pl.multiple_of(h * half, half)
                lhs = jnp.concatenate([pr[k, z, s, pl.ds(off, half), :] for z in range(NR)], axis=1)
                hi = jnp.concatenate([q_hi[s, z] for z in range(NR)], axis=0)
                lo = jnp.concatenate([q_lo[s, z] for z in range(NR)], axis=0)
                total = dot(lhs, hi, ((1,), (0,))) + dot(lhs, lo, ((1,), (0,)))
                where = pl.ds(pl.multiple_of(k * wide + h * half, half), half)
                diag_v[where, s * wide:(s + 1) * wide] = diag_v[where, s * wide:(s + 1) * wide] - total
        block = pl.ds(k * wide, wide)
        pltpu.make_async_copy(diag_v.at[block], diag_out.at[block], do_sem.at[k]).start()

    for copy in sends:
        copy.wait_send()
    for t in range(NR):
        z = lax.rem(r + t * turn + 8, NR)
        for s in range(NS):
            @pl.when(hop < 3)
            def _():
                chain_copy(z, t, s).wait_send()

            sib_copy(z, t, s).wait_send()
    for k in range(2):
        block = pl.ds(k * wide, wide)
        pltpu.make_async_copy(diag_v.at[block], diag_out.at[block], do_sem.at[k]).wait()


def local_kernel(factor_panel, ancestor_inv, diag_inverse, structure):
    rows, width = factor_panel.shape
    wide = width // NS
    acols = ancestor_inv.shape[1]
    dma = pltpu.SemaphoreType.DMA
    bf16, f32 = jnp.bfloat16, jnp.float32
    vmem = pl.BlockSpec(memory_space=pltpu.VMEM)
    return pl.pallas_call(
        kernel,
        out_shape=(
            jax.ShapeDtypeStruct((rows, width), f32),
            jax.ShapeDtypeStruct(diag_inverse.shape, f32),
        ),
        in_specs=[pl.BlockSpec(memory_space=pltpu.SMEM), vmem, vmem, pl.BlockSpec(memory_space=pl.ANY)],
        out_specs=(vmem, pl.BlockSpec(memory_space=pl.ANY)),
        scratch_shapes=[
            pltpu.VMEM((NR, NS, wide, rows), bf16),
            pltpu.VMEM((2, NR, NS, wide, rows), bf16),
            pltpu.VMEM((NC, NR, rows, acols), f32),
            pltpu.VMEM((NC, NR, rows, acols), bf16),
            pltpu.VMEM((NC, NR, rows, acols), bf16),
            pltpu.VMEM((NS, NR, rows, wide), bf16),
            pltpu.VMEM((NS, NR, rows, wide), bf16),
            pltpu.VMEM(diag_inverse.shape, f32),
            dma((NR - 1, NS)), dma((NR, NS)), dma((NR - 1,)), dma((NR,)),
            dma((3,)), dma((3,)), dma((4,)), dma((4,)),
            dma((NR, NS)), dma((NR, NS)), dma((NR, NS)), dma((NR, NS)),
            dma((NR, NS)), dma, dma((2,)),
        ],
        compiler_params=pltpu.CompilerParams(
            collective_id=0, has_side_effects=True, vmem_limit_bytes=48 << 20),
    )(structure, factor_panel, ancestor_inv, diag_inverse)


def solution(mesh):
    placed = (P("row", "col"), P("row", "col"), P("row", "col"), P())

    def body(factor_panel, ancestor_inv, diag_inverse, structure):
        rows, width = factor_panel.shape
        fits = (mesh.shape["row"], mesh.shape["col"]) == (NR, NC) and rows == B
        fits = fits and diag_inverse.shape[0] * NS == 2 * width
        return (local_kernel if fits else local)(factor_panel, ancestor_inv, diag_inverse, structure)

    return jax.shard_map(
        body,
        mesh=mesh,
        in_specs=placed,
        out_specs=(P("row", "col"), P("row", "col")),
        check_vma=False,
    )
```

```python
import functools

import jax
import jax.numpy as jnp
from jax import lax
from jax.experimental import pallas as pl
from jax.experimental.pallas import tpu as pltpu
from jax.sharding import PartitionSpec as P

B = 256
NS = 2
NR = 4
NC = 8
MESH = pl.DeviceIdType.MESH


def local(factor_panel, ancestor_inv, diag_inverse, structure):
    rows_dev, width_dev = factor_panel.shape
    per_block = width_dev // NS
    row_index = lax.axis_index("row")
    keep_tiles = jnp.repeat(structure, B, axis=1)
    keep_own = lax.dynamic_slice_in_dim(keep_tiles, row_index * rows_dev, rows_dev, 1)
    keep_cols = jnp.repeat(keep_own.T, per_block, axis=1)
    lhat_local = jnp.where(keep_cols == 1, factor_panel, jnp.zeros_like(factor_panel))
    column = lax.all_gather(lhat_local, "row", axis=0, tiled=True)
    sigma_rows = lax.all_gather(ancestor_inv, "col", axis=1, tiled=True)
    column_wide = column.astype(jnp.float32)
    running = jnp.dot(sigma_rows, column_wide, precision=lax.Precision.HIGHEST)
    inverse_panel = jnp.where(keep_cols == 1, -running, jnp.zeros_like(running))
    rows_all = lax.all_gather(lhat_local, "col", axis=1, tiled=True)
    block_count = rows_all.shape[1] // width_dev
    rows_cube = rows_all.reshape(rows_dev, block_count, NS, per_block)
    lhat_members = [
        rows_cube[:, :, member, :].reshape(rows_dev, block_count * per_block).astype(jnp.float32)
        for member in range(NS)
    ]
    pieces = []
    for member in range(NS):
        window = lhat_members[member]
        target = inverse_panel[:, member * per_block : (member + 1) * per_block]
        pieces.append(
            lax.dot_general(
                window,
                target,
                (((0,), (0,)), ((), ())),
                precision=lax.Precision.HIGHEST,
                preferred_element_type=jnp.float32,
            )
        )
    update = lax.psum_scatter(
        jnp.concatenate(pieces, axis=1), "row", scatter_dimension=0, tiled=True
    )
    diag_sigma = diag_inverse - update
    return (inverse_panel, diag_sigma)


def kernel(structure, factor, anc, diag_in, panel_out, diag_out,
           lt, pr, asl, a_hi, a_lo, q_hi, q_lo,
           zl_send, zl_recv, za_send, za_recv, ra_send, ra_recv, sa_send, sa_recv,
           pc_send, pc_recv, ps_send, ps_recv, lc_sem, di_sem):
    r = lax.axis_index("row")
    c = lax.axis_index("col")
    wide = factor.shape[1] // NS
    core = lax.rem(c, 2)
    pos = c // 2
    step = 1 - 2 * core

    def gray(p):
        y = p // 2
        return 2 * y + lax.rem(lax.rem(p, 2) + y, 2)

    q_me = gray(pos)
    hop = lax.rem((q_me - gray(r)) * step + 8, 4)

    def ring_col(k, kind):
        return gray(lax.rem(q_me + k * step + 8, 4)) * 2 + kind

    nxt, prv = ring_col(1, core), ring_col(-1, core)
    sib = pos * 2 + 1 - core
    has = (r < NR - 1, r > 0)
    to = ((lax.rem(r + 1, NR), c), (lax.rem(r + NR - 1, NR), c))
    order = [r, r + 1 - 2 * (r // 3), lax.rem(r + 2, 3) - r // 3, 3 * (1 - r // 2)]

    barrier = pltpu.get_barrier_semaphore()
    for dev in ((r, nxt), (r, prv), (r, sib)) + to:
        pl.semaphore_signal(barrier, inc=1, device_id=dev, device_id_type=MESH)

    diag_load = pltpu.make_async_copy(diag_in, diag_out, di_sem)
    diag_load.start()
    asl[c, r] = anc[...]
    for s in range(NS):
        part = factor[:, s * wide:(s + 1) * wide]
        kept = jnp.where(structure[s, r] == 1, part.astype(jnp.float32), 0.0)
        lt[r, s] = kept.T.astype(jnp.bfloat16)
    pl.semaphore_wait(barrier, 5)

    def remote(ref, send, recv, dev, src=None):
        return pltpu.make_async_remote_copy(
            src_ref=ref if src is None else src, dst_ref=ref, send_sem=send, recv_sem=recv,
            device_id=dev, device_id_type=MESH)

    sends = []

    def go(cond, copy):
        sends.append((cond, copy))
        if cond is None:
            copy.start()
        else:
            @pl.when(cond)
            def _():
                copy.start()

    def row_send(j, s=None):
        for way in range(2):
            z = (r - j) if way == 0 else (r + j)
            there = (z >= 0) & (z < NR) & has[way]
            z = lax.rem(z + NR, NR)
            if s is None:
                copy = remote(asl.at[c, z], za_send.at[way, j], za_recv.at[way, j], to[way])
            else:
                copy = remote(lt.at[z, s], zl_send.at[way, j, s], zl_recv.at[way, j, s], to[way])
            go(there, copy)

    def row_wait(j, s=None):
        for way in range(2):
            z = (r - 1 - j) if way == 0 else (r + 1 + j)
            there = (z >= 0) & (z < NR)
            z = lax.rem(z + NR, NR)

            @pl.when(there)
            def _():
                if s is None:
                    remote(asl.at[c, z], za_send.at[way, j], za_recv.at[way, j], to[way]).wait_recv()
                else:
                    remote(lt.at[z, s], zl_send.at[way, j, s], zl_recv.at[way, j, s], to[way]).wait_recv()

    def chain_copy(t, s, src=None):
        return remote(pr.at[core, order[t], s], pc_send.at[t, s], pc_recv.at[t, s], (r, nxt), src)

    def sib_copy(t, s, src=None):
        return remote(pr.at[core, order[t], s], ps_send.at[t, s], ps_recv.at[t, s], (r, sib), src)

    def own_copy(t, s):
        z = order[t]
        return pltpu.make_async_copy(lt.at[z, s], pr.at[core, z, s], lc_sem.at[t, s])

    def chain(t, s, low, high):
        if low == 0:
            @pl.when(hop == 0)
            def _():
                src = lt.at[order[t], s]
                chain_copy(t, s, src).start()
                sib_copy(t, s, src).start()
                own_copy(t, s).start()

        if high > 0:
            @pl.when((hop >= max(low, 1)) & (hop <= high))
            def _():
                chain_copy(t, s).wait_recv()

                @pl.when(hop < 3)
                def _():
                    chain_copy(t, s).start()

                sib_copy(t, s).start()

    def ring(t, k):
        part = asl.at[ring_col(-k, core), order[t]]
        if k > 0:
            remote(part, ra_send.at[t, k - 1], ra_recv.at[t, k - 1], (r, nxt)).wait_recv()
        if k < 3:
            go(None, remote(part, ra_send.at[t, k], ra_recv.at[t, k], (r, nxt)))
        go(None, remote(part, sa_send.at[t, k], sa_recv.at[t, k], (r, sib)))

    row_send(0)
    chain(0, 0, 0, 0)
    ring(0, 0)
    row_wait(0)
    row_send(1)
    row_send(0, 0)
    ring(1, 0)
    chain(0, 0, 1, 1)
    chain(0, 1, 0, 0)
    ring(0, 1)
    row_wait(1)
    row_send(2)
    row_send(0, 1)
    ring(2, 0)
    ring(0, 2)
    ring(1, 1)
    chain(0, 0, 2, 2)
    chain(0, 1, 1, 1)
    ring(0, 3)
    ring(1, 2)
    chain(0, 0, 3, 3)
    row_wait(0, 0)
    row_send(1, 0)
    chain(1, 0, 0, 0)
    chain(0, 1, 2, 2)
    ring(2, 1)
    ring(1, 3)
    row_wait(2)
    ring(3, 0)
    ring(2, 2)
    chain(1, 0, 1, 1)
    chain(0, 1, 3, 3)
    row_wait(0, 1)
    row_send(1, 1)
    chain(1, 1, 0, 0)
    chain(1, 0, 2, 2)
    ring(3, 1)
    ring(2, 3)
    row_wait(1, 0)
    row_send(2, 0)
    chain(2, 0, 0, 0)
    chain(1, 1, 1, 1)
    chain(1, 0, 3, 3)
    ring(3, 2)
    chain(2, 0, 1, 1)
    chain(1, 1, 2, 2)
    row_wait(1, 1)
    row_send(2, 1)
    chain(2, 1, 0, 0)
    ring(3, 3)
    chain(1, 1, 3, 3)
    chain(2, 0, 2, 2)
    for t in range(NR):
        for k in range(4):
            other = asl.at[ring_col(k, 1 - core), order[t]]
            remote(other, sa_send.at[t, k], sa_recv.at[t, k], (r, sib)).wait_recv()

    @pl.loop(0, NC)
    def _(col):
        for z in range(NR):
            a = asl[col, z]
            hi = a.astype(jnp.bfloat16)
            a_hi[col, z] = hi
            a_lo[col, z] = (a - hi.astype(jnp.float32)).astype(jnp.bfloat16)

    chain(2, 1, 1, 1)
    chain(2, 0, 3, 3)

    def dot(a, b, dims):
        return lax.dot_general(a, b, (dims, ((), ())), preferred_element_type=jnp.float32)

    def panel(s):
        @pl.loop(0, NR)
        def _(z):
            rhs = jnp.concatenate([lt[b, s] for b in range(NR)], axis=1)
            hi = jnp.concatenate([a_hi[col, z] for col in range(NC)], axis=1)
            lo = jnp.concatenate([a_lo[col, z] for col in range(NC)], axis=1)
            total = dot(hi, rhs, ((1,), (1,))) + dot(lo, rhs, ((1,), (1,)))
            total = jnp.where(structure[s, z] == 1, -total, 0.0)
            top = total.astype(jnp.bfloat16)
            q_hi[s, z] = top
            q_lo[s, z] = (total - top.astype(jnp.float32)).astype(jnp.bfloat16)

            @pl.when(z == r)
            def _():
                panel_out[:, s * wide:(s + 1) * wide] = total

    def arrived(t, s):
        @pl.when(hop == 0)
        def _():
            own_copy(t, s).wait()

        remote(pr.at[1 - core, order[t], s], ps_send.at[t, s], ps_recv.at[t, s], (r, sib)).wait_recv()

    half = wide // 2

    def update(s, ts, first=0, last=4):
        @pl.loop(first, last)
        def _(it):
            k = it // 2
            off = pl.multiple_of((it - 2 * k) * half, half)
            where = pl.ds(pl.multiple_of(it * half, half), half)
            lhs = jnp.concatenate([pr[k, order[t], s, pl.ds(off, half), :] for t in ts], axis=1)
            hi = jnp.concatenate([q_hi[s, order[t]] for t in ts], axis=0)
            lo = jnp.concatenate([q_lo[s, order[t]] for t in ts], axis=0)
            total = dot(lhs, hi, ((1,), (0,))) + dot(lhs, lo, ((1,), (0,)))
            here = slice(s * wide, (s + 1) * wide)
            diag_out[where, here] = diag_out[where, here] - total

    row_wait(2, 0)
    chain(3, 0, 0, 0)
    chain(2, 1, 2, 2)
    panel(0)
    chain(3, 0, 1, 1)
    chain(2, 1, 3, 3)
    chain(3, 0, 2, 2)
    row_wait(2, 1)
    chain(3, 1, 0, 0)
    diag_load.wait()
    panel(1)
    chain(3, 1, 1, 1)
    chain(3, 0, 3, 3)
    for t in range(NR):
        arrived(t, 0)
    update(0, (0, 1, 2, 3), 0, 2)
    chain(3, 1, 2, 2)
    update(0, (0, 1, 2, 3), 2, 4)
    for t in range(3):
        arrived(t, 1)
    update(1, (0, 1, 2), 0, 2)
    chain(3, 1, 3, 3)
    update(1, (0, 1, 2), 2, 4)
    arrived(3, 1)
    update(1, (3,))

    for cond, copy in sends:
        if cond is None:
            copy.wait_send()
        else:
            pl.when(cond)(copy.wait_send)
    for t in range(NR):
        for s in range(NS):
            @pl.when(hop < 3)
            def _():
                chain_copy(t, s).wait_send()

            sib_copy(t, s).wait_send()


def local_kernel(factor_panel, ancestor_inv, diag_inverse, structure):
    rows, width = factor_panel.shape
    wide = width // NS
    acols = ancestor_inv.shape[1]
    dma = pltpu.SemaphoreType.DMA
    bf16, f32 = jnp.bfloat16, jnp.float32
    vmem = pl.BlockSpec(memory_space=pltpu.VMEM)
    return pl.pallas_call(
        kernel,
        out_shape=(
            jax.ShapeDtypeStruct((rows, width), f32),
            jax.ShapeDtypeStruct(diag_inverse.shape, f32),
        ),
        in_specs=[pl.BlockSpec(memory_space=pltpu.SMEM), vmem, vmem, pl.BlockSpec(memory_space=pl.ANY)],
        out_specs=(vmem, vmem),
        scratch_shapes=[
            pltpu.VMEM((NR, NS, wide, rows), bf16),
            pltpu.VMEM((2, NR, NS, wide, rows), bf16),
            pltpu.VMEM((NC, NR, rows, acols), f32),
            pltpu.VMEM((NC, NR, rows, acols), bf16),
            pltpu.VMEM((NC, NR, rows, acols), bf16),
            pltpu.VMEM((NS, NR, rows, wide), bf16),
            pltpu.VMEM((NS, NR, rows, wide), bf16),
            dma((2, NR - 1, NS)), dma((2, NR - 1, NS)), dma((2, NR - 1)), dma((2, NR - 1)),
            dma((NR, 3)), dma((NR, 3)), dma((NR, 4)), dma((NR, 4)),
            dma((NR, NS)), dma((NR, NS)), dma((NR, NS)), dma((NR, NS)),
            dma((NR, NS)), dma,
        ],
        compiler_params=pltpu.CompilerParams(
            collective_id=0, has_side_effects=True, vmem_limit_bytes=48 << 20),
    )(structure, factor_panel, ancestor_inv, diag_inverse)


def solution(mesh):
    placed = (P("row", "col"), P("row", "col"), P("row", "col"), P())

    def body(factor_panel, ancestor_inv, diag_inverse, structure):
        rows, width = factor_panel.shape
        fits = (mesh.shape["row"], mesh.shape["col"]) == (NR, NC) and rows == B
        fits = fits and diag_inverse.shape[0] * NS == 2 * width
        return (local_kernel if fits else local)(factor_panel, ancestor_inv, diag_inverse, structure)

    return jax.shard_map(
        body,
        mesh=mesh,
        in_specs=placed,
        out_specs=(P("row", "col"), P("row", "col")),
        check_vma=False,
    )
```

```python
import functools

import jax
import jax.numpy as jnp
from jax import lax
from jax.experimental import pallas as pl
from jax.experimental.pallas import tpu as pltpu
from jax.sharding import PartitionSpec as P

B = 256
NS = 2
NR = 4
NC = 8
SUB = 4
MESH = pl.DeviceIdType.MESH


def local(factor_panel, ancestor_inv, diag_inverse, structure):
    rows_dev, width_dev = factor_panel.shape
    per_block = width_dev // NS
    row_index = lax.axis_index("row")
    keep_tiles = jnp.repeat(structure, B, axis=1)
    keep_own = lax.dynamic_slice_in_dim(keep_tiles, row_index * rows_dev, rows_dev, 1)
    keep_cols = jnp.repeat(keep_own.T, per_block, axis=1)
    lhat_local = jnp.where(keep_cols == 1, factor_panel, jnp.zeros_like(factor_panel))
    column = lax.all_gather(lhat_local, "row", axis=0, tiled=True)
    sigma_rows = lax.all_gather(ancestor_inv, "col", axis=1, tiled=True)
    column_wide = column.astype(jnp.float32)
    running = jnp.dot(sigma_rows, column_wide, precision=lax.Precision.HIGHEST)
    inverse_panel = jnp.where(keep_cols == 1, -running, jnp.zeros_like(running))
    rows_all = lax.all_gather(lhat_local, "col", axis=1, tiled=True)
    block_count = rows_all.shape[1] // width_dev
    rows_cube = rows_all.reshape(rows_dev, block_count, NS, per_block)
    lhat_members = [
        rows_cube[:, :, member, :].reshape(rows_dev, block_count * per_block).astype(jnp.float32)
        for member in range(NS)
    ]
    pieces = []
    for member in range(NS):
        window = lhat_members[member]
        target = inverse_panel[:, member * per_block : (member + 1) * per_block]
        pieces.append(
            lax.dot_general(
                window,
                target,
                (((0,), (0,)), ((), ())),
                precision=lax.Precision.HIGHEST,
                preferred_element_type=jnp.float32,
            )
        )
    update = lax.psum_scatter(
        jnp.concatenate(pieces, axis=1), "row", scatter_dimension=0, tiled=True
    )
    diag_sigma = diag_inverse - update
    return (inverse_panel, diag_sigma)


def kernel(structure, factor, anc, diag_in, panel_out, diag_out,
           lt, pr, asl, a_hi, a_lo, q_sum, q_hi, q_lo,
           zl_send, zl_recv, za_send, za_recv, ra_send, ra_recv, sa_send, sa_recv,
           pc_send, pc_recv, ps_send, ps_recv, lc_sem, di_sem):
    r = lax.axis_index("row")
    c = lax.axis_index("col")
    wide = factor.shape[1] // NS
    core = lax.rem(c, 2)
    pos = c // 2
    step = 1 - 2 * core

    def gray(p):
        y = p // 2
        return 2 * y + lax.rem(lax.rem(p, 2) + y, 2)

    q_me = gray(pos)
    hop = lax.rem((q_me - gray(r)) * step + 8, 4)

    def ring_col(k, kind):
        return gray(lax.rem(q_me + k * step + 8, 4)) * 2 + kind

    nxt, prv = ring_col(1, core), ring_col(-1, core)
    sib = pos * 2 + 1 - core
    has = (r < NR - 1, r > 0)
    to = ((lax.rem(r + 1, NR), c), (lax.rem(r + NR - 1, NR), c))
    order = [r, r + 1 - 2 * (r // 3), lax.rem(r + 2, 3) - r // 3, 3 * (1 - r // 2)]

    barrier = pltpu.get_barrier_semaphore()
    for dev in ((r, nxt), (r, prv), (r, sib)) + to:
        pl.semaphore_signal(barrier, inc=1, device_id=dev, device_id_type=MESH)

    diag_load = pltpu.make_async_copy(diag_in, diag_out, di_sem)
    diag_load.start()
    asl[c, r] = anc[...]
    for s in range(NS):
        part = factor[:, s * wide:(s + 1) * wide]
        kept = jnp.where(structure[s, r] == 1, part.astype(jnp.float32), 0.0)
        lt[r, s] = kept.T.astype(jnp.bfloat16)
    pl.semaphore_wait(barrier, 5)

    def remote(ref, send, recv, dev, src=None):
        return pltpu.make_async_remote_copy(
            src_ref=ref if src is None else src, dst_ref=ref, send_sem=send, recv_sem=recv,
            device_id=dev, device_id_type=MESH)

    sends = []

    def go(cond, copy):
        sends.append((cond, copy))
        if cond is None:
            copy.start()
        else:
            @pl.when(cond)
            def _():
                copy.start()

    def row_send(j, s=None):
        for way in range(2):
            z = (r - j) if way == 0 else (r + j)
            there = (z >= 0) & (z < NR) & has[way]
            z = lax.rem(z + NR, NR)
            if s is None:
                copy = remote(asl.at[c, z], za_send.at[way, j], za_recv.at[way, j], to[way])
            else:
                copy = remote(lt.at[z, s], zl_send.at[way, j, s], zl_recv.at[way, j, s], to[way])
            go(there, copy)

    def row_wait(j, s=None):
        for way in range(2):
            z = (r - 1 - j) if way == 0 else (r + 1 + j)
            there = (z >= 0) & (z < NR)
            z = lax.rem(z + NR, NR)

            @pl.when(there)
            def _():
                if s is None:
                    remote(asl.at[c, z], za_send.at[way, j], za_recv.at[way, j], to[way]).wait_recv()
                else:
                    remote(lt.at[z, s], zl_send.at[way, j, s], zl_recv.at[way, j, s], to[way]).wait_recv()

    def parts(t):
        count = SUB if t == NR - 1 else 1
        return [(i, pl.ds(i * (wide // count), wide // count)) for i in range(count)]

    def chain_copy(t, s, i, cut, src=None):
        return remote(pr.at[core, order[t], s, cut], pc_send.at[t, s, i], pc_recv.at[t, s, i], (r, nxt), src)

    def sib_copy(t, s, i, cut, src=None):
        return remote(pr.at[core, order[t], s, cut], ps_send.at[t, s, i], ps_recv.at[t, s, i], (r, sib), src)

    def own_copy(t, s):
        z = order[t]
        return pltpu.make_async_copy(lt.at[z, s], pr.at[core, z, s], lc_sem.at[t, s])

    def chain(t, s, low, high):
        if low == 0:
            @pl.when(hop == 0)
            def _():
                for i, cut in parts(t):
                    src = lt.at[order[t], s, cut]
                    chain_copy(t, s, i, cut, src).start()
                    sib_copy(t, s, i, cut, src).start()
                own_copy(t, s).start()

        if high > 0:
            @pl.when((hop >= max(low, 1)) & (hop <= high))
            def _():
                for i, cut in parts(t):
                    chain_copy(t, s, i, cut).wait_recv()

                    @pl.when(hop < 3)
                    def _():
                        chain_copy(t, s, i, cut).start()

                    sib_copy(t, s, i, cut).start()

    def ring(t, k):
        part = asl.at[ring_col(-k, core), order[t]]
        if k > 0:
            remote(part, ra_send.at[t, k - 1], ra_recv.at[t, k - 1], (r, nxt)).wait_recv()
        if k < 3:
            go(None, remote(part, ra_send.at[t, k], ra_recv.at[t, k], (r, nxt)))
        go(None, remote(part, sa_send.at[t, k], sa_recv.at[t, k], (r, sib)))

    def dot(a, b, dims):
        return lax.dot_general(a, b, (dims, ((), ())), preferred_element_type=jnp.float32)

    def product(s, z, ts):
        rhs = jnp.concatenate([lt[order[t], s] for t in ts], axis=1)
        cols = [2 * order[t] + i for t in ts for i in range(2)]
        hi = jnp.concatenate([a_hi[col, z] for col in cols], axis=1)
        lo = jnp.concatenate([a_lo[col, z] for col in cols], axis=1)
        return dot(hi, rhs, ((1,), (1,))) + dot(lo, rhs, ((1,), (1,)))

    def panel_start(s):
        @pl.loop(0, NR)
        def _(z):
            q_sum[s, z] = product(s, z, (0, 1, 2))

    def panel_end(s):
        @pl.loop(0, NR)
        def _(z):
            total = product(s, z, (0, 1, 2, 3))
            total = jnp.where(structure[s, z] == 1, -total, 0.0)
            top = total.astype(jnp.bfloat16)
            q_hi[s, z] = top
            q_lo[s, z] = (total - top.astype(jnp.float32)).astype(jnp.bfloat16)

            @pl.when(z == r)
            def _():
                panel_out[:, s * wide:(s + 1) * wide] = total

    row_send(0)
    chain(0, 0, 0, 0)
    ring(0, 0)
    row_wait(0)
    row_send(1)
    row_send(0, 0)
    ring(1, 0)
    chain(0, 0, 1, 1)
    chain(0, 1, 0, 0)
    ring(0, 1)
    row_wait(1)
    row_send(2)
    row_send(0, 1)
    ring(2, 0)
    ring(0, 2)
    ring(1, 1)
    chain(0, 0, 2, 2)
    chain(0, 1, 1, 1)
    ring(0, 3)
    ring(1, 2)
    chain(0, 0, 3, 3)
    row_wait(0, 0)
    row_send(1, 0)
    chain(1, 0, 0, 0)
    chain(0, 1, 2, 2)
    ring(2, 1)
    ring(1, 3)
    row_wait(2)
    ring(3, 0)
    ring(2, 2)
    chain(1, 0, 1, 1)
    chain(0, 1, 3, 3)
    row_wait(0, 1)
    row_send(1, 1)
    chain(1, 1, 0, 0)
    chain(1, 0, 2, 2)
    ring(3, 1)
    ring(2, 3)
    row_wait(1, 0)
    row_send(2, 0)
    chain(2, 0, 0, 0)
    chain(1, 1, 1, 1)
    chain(1, 0, 3, 3)
    ring(3, 2)
    chain(2, 0, 1, 1)
    chain(1, 1, 2, 2)
    row_wait(1, 1)
    row_send(2, 1)
    chain(2, 1, 0, 0)
    ring(3, 3)
    chain(1, 1, 3, 3)
    chain(2, 0, 2, 2)
    for t in range(NR):
        for k in range(4):
            other = asl.at[ring_col(k, 1 - core), order[t]]
            remote(other, sa_send.at[t, k], sa_recv.at[t, k], (r, sib)).wait_recv()

    @pl.loop(0, NC)
    def _(col):
        for z in range(NR):
            a = asl[col, z]
            hi = a.astype(jnp.bfloat16)
            a_hi[col, z] = hi
            a_lo[col, z] = (a - hi.astype(jnp.float32)).astype(jnp.bfloat16)

    chain(2, 1, 1, 1)
    chain(2, 0, 3, 3)
    chain(2, 1, 2, 2)

    def arrived(t, s):
        @pl.when(hop == 0)
        def _():
            own_copy(t, s).wait()

        for i, cut in parts(t):
            remote(pr.at[1 - core, order[t], s, cut], ps_send.at[t, s, i], ps_recv.at[t, s, i], (r, sib)).wait_recv()

    half = wide // 2

    def update(s, ts, first=0, last=4):
        @pl.loop(first, last)
        def _(it):
            k = it // 2
            off = pl.multiple_of((it - 2 * k) * half, half)
            where = pl.ds(pl.multiple_of(it * half, half), half)
            lhs = jnp.concatenate([pr[k, order[t], s, pl.ds(off, half), :] for t in ts], axis=1)
            hi = jnp.concatenate([q_hi[s, order[t]] for t in ts], axis=0)
            lo = jnp.concatenate([q_lo[s, order[t]] for t in ts], axis=0)
            total = dot(lhs, hi, ((1,), (0,))) + dot(lhs, lo, ((1,), (0,)))
            here = slice(s * wide, (s + 1) * wide)
            diag_out[where, here] = diag_out[where, here] - total

    diag_load.wait()
    row_wait(2, 0)
    chain(3, 0, 0, 0)
    chain(2, 1, 3, 3)
    panel_end(0)
    chain(3, 0, 1, 1)
    row_wait(2, 1)
    chain(3, 1, 0, 0)
    chain(3, 0, 2, 2)
    panel_end(1)
    chain(3, 1, 1, 1)
    chain(3, 0, 3, 3)
    for t in range(NR):
        arrived(t, 0)
    update(0, (0, 1, 2, 3), 0, 2)
    chain(3, 1, 2, 2)
    update(0, (0, 1, 2, 3), 2, 4)
    for t in range(3):
        arrived(t, 1)
    update(1, (0, 1, 2))
    chain(3, 1, 3, 3)
    arrived(3, 1)
    update(1, (3,))

    for cond, copy in sends:
        if cond is None:
            copy.wait_send()
        else:
            pl.when(cond)(copy.wait_send)
    for t in range(NR):
        for s in range(NS):
            for i, cut in parts(t):
                @pl.when(hop < 3)
                def _():
                    chain_copy(t, s, i, cut).wait_send()

                sib_copy(t, s, i, cut).wait_send()


def local_kernel(factor_panel, ancestor_inv, diag_inverse, structure):
    rows, width = factor_panel.shape
    wide = width // NS
    acols = ancestor_inv.shape[1]
    dma = pltpu.SemaphoreType.DMA
    bf16, f32 = jnp.bfloat16, jnp.float32
    vmem = pl.BlockSpec(memory_space=pltpu.VMEM)
    return pl.pallas_call(
        kernel,
        out_shape=(
            jax.ShapeDtypeStruct((rows, width), f32),
            jax.ShapeDtypeStruct(diag_inverse.shape, f32),
        ),
        in_specs=[pl.BlockSpec(memory_space=pltpu.SMEM), vmem, vmem, pl.BlockSpec(memory_space=pl.ANY)],
        out_specs=(vmem, vmem),
        scratch_shapes=[
            pltpu.VMEM((NR, NS, wide, rows), bf16),
            pltpu.VMEM((2, NR, NS, wide, rows), bf16),
            pltpu.VMEM((NC, NR, rows, acols), f32),
            pltpu.VMEM((NC, NR, rows, acols), bf16),
            pltpu.VMEM((NC, NR, rows, acols), bf16),
            pltpu.VMEM((NS, NR, rows, wide), f32),
            pltpu.VMEM((NS, NR, rows, wide), bf16),
            pltpu.VMEM((NS, NR, rows, wide), bf16),
            dma((2, NR - 1, NS)), dma((2, NR - 1, NS)), dma((2, NR - 1)), dma((2, NR - 1)),
            dma((NR, 3)), dma((NR, 3)), dma((NR, 4)), dma((NR, 4)),
            dma((NR, NS, SUB)), dma((NR, NS, SUB)), dma((NR, NS, SUB)), dma((NR, NS, SUB)),
            dma((NR, NS)), dma,
        ],
        compiler_params=pltpu.CompilerParams(
            collective_id=0, has_side_effects=True, vmem_limit_bytes=48 << 20),
    )(structure, factor_panel, ancestor_inv, diag_inverse)


def solution(mesh):
    placed = (P("row", "col"), P("row", "col"), P("row", "col"), P())

    def body(factor_panel, ancestor_inv, diag_inverse, structure):
        rows, width = factor_panel.shape
        fits = (mesh.shape["row"], mesh.shape["col"]) == (NR, NC) and rows == B
        fits = fits and diag_inverse.shape[0] * NS == 2 * width
        return (local_kernel if fits else local)(factor_panel, ancestor_inv, diag_inverse, structure)

    return jax.shard_map(
        body,
        mesh=mesh,
        in_specs=placed,
        out_specs=(P("row", "col"), P("row", "col")),
        check_vma=False,
    )
```
